256 devices in a mesh: lon: 32 (over z, y_lo, core), lat: 8 (over x, y_hi).
Axes of the slice: x: 4, y: 4 (y_hi: 2, y_lo: 2; y = y_hi * 2 + y_lo), z: 8, core: 2. Of those that a mesh axis runs over, the one named last changes fastest.
Arguments:
- embeddings: bfloat16 [512, 2048, 128], P('lat', 'lon'), may hold values from -400 to 400
- query_owner: int32 [2, 64], replicated, may hold values from 0 to 255
- query_row: int32 [2, 64], replicated, may hold values from 0 to 59
- query_col: int32 [2, 64], replicated, may hold values from 0 to 59
Outputs:
- scores: float32 [512, 2048, 128], P('lat', 'lon')
The draws below stay inside these ranges and needn't reach their ends.
Inputs may be any that keep to these rules, and one draw needn't show every extreme that they name: `query_row`: the exemplar lies inside its owner's tile. `query_col`: the exemplar lies inside its owner's tile.
All inputs are finite; a program needn't handle non-finite values.
Results may differ from the reference program's by a relative error of at most 0.0029.
Values may be sent and summed in bfloat16 or wider, within the bound.
A program may use at most 128 MiB of HBM per device.

```python
import jax
import jax.numpy as jnp
from jax import lax

C = 128
PQ = 64
PANELS = 2
TH = 64
TW = 64
QUERIES = 128
ROWS = 512
COLS = 2048
N_LON = 32
N_LAT = 8
DEVICES = 256


def draw_embeddings(key, part):
    key_base = jax.random.fold_in(key, 11)
    key_cell = jax.random.fold_in(key, 12)
    key_chan = jax.random.fold_in(key, 13)
    base = jnp.clip(jax.random.normal(key_base, (ROWS, COLS, C), jnp.float32), -4.0, 4.0)
    cell_scale = 10.0 ** jax.random.uniform(key_cell, (ROWS, COLS, 1), jnp.float32, 0.0, 1.0)
    chan_scale = 10.0 ** jax.random.uniform(key_chan, (C,), jnp.float32, 0.0, 1.0)
    return (base * cell_scale * chan_scale).astype(jnp.bfloat16)


def place_ends(result, own_key, low, top_value):
    shape = result.shape
    place = [jax.random.randint(jax.random.fold_in(own_key, axis), (), 0, shape[axis]) for axis in range(len(shape))]
    result = result.at[tuple(place)].set(low)
    longest = shape.index(max(shape))
    place[longest] = (place[longest] + 1) % shape[longest]
    return result.at[tuple(place)].set(top_value)


def setup_inputs(seed: int = 0) -> dict:
    key_of = jax.random.split(jax.random.key(seed), 5)
    embeddings = draw_embeddings(jax.random.fold_in(key_of[4], 71), 0)
    query_owner = place_ends(jax.random.randint(key_of[1], (PANELS, PQ), 0, DEVICES), jax.random.fold_in(key_of[1], 1), 0, DEVICES - 1).astype(jnp.int32)
    query_row = place_ends(jax.random.randint(key_of[2], (PANELS, PQ), 0, TH - 4), jax.random.fold_in(key_of[2], 1), 0, (TH - 4) - 1).astype(jnp.int32)
    query_col = place_ends(jax.random.randint(key_of[3], (PANELS, PQ), 0, TW - 4), jax.random.fold_in(key_of[3], 1), 0, (TW - 4) - 1).astype(jnp.int32)
    return dict(embeddings=embeddings, query_owner=query_owner, query_row=query_row, query_col=query_col)


def window_table(embeddings, query_owner, query_row, query_col):
    owner = query_owner.reshape(-1).astype(jnp.int32)
    band = owner // N_LON
    strip = owner % N_LON
    row_start = (band * TH + query_row.reshape(-1)).astype(jnp.int32)
    col_start = (strip * TW + query_col.reshape(-1)).astype(jnp.int32)

    def take(row_first, col_first):
        zero = jnp.zeros((), jnp.int32)
        return lax.dynamic_slice(embeddings, (row_first, col_first, zero), (5, 5, C))
    return jax.vmap(take, out_axes=3)(row_start, col_start)

def reference(embeddings, query_owner, query_row, query_col):
    patch = window_table(embeddings, query_owner, query_row, query_col).astype(jnp.float32)
    mean_sq = lax.optimization_barrier(jnp.mean(patch * patch, axis=(0, 1, 2)))
    queries = (patch * lax.rsqrt(mean_sq + 1e-05)).astype(jnp.bfloat16)
    wrapped = jnp.concatenate([embeddings[:, -2:], embeddings, embeddings[:, :2]], axis=1)
    extended = jnp.pad(wrapped, ((2, 2), (0, 0), (0, 0)))

    def one_band(band):
        zero = jnp.zeros((), jnp.int32)
        block = lax.dynamic_slice(extended, ((band * TH).astype(jnp.int32), zero, zero), (TH + 4, COLS + 4, C))
        total = jnp.zeros((TH * COLS, QUERIES), jnp.float32)
        for shift_y in range(5):
            for shift_x in range(5):
                slab = block[shift_y:shift_y + TH, shift_x:shift_x + COLS, :].reshape(TH * COLS, C)
                total = total + jnp.dot(slab, queries[shift_y, shift_x], preferred_element_type=jnp.float32)
        squares = lax.optimization_barrier(jnp.sum(jnp.square(block.astype(jnp.float32)), axis=2))
        box_sum = jnp.zeros((TH, COLS), jnp.float32)
        for shift_y in range(5):
            for shift_x in range(5):
                box_sum = box_sum + squares[shift_y:shift_y + TH, shift_x:shift_x + COLS]
        energy = box_sum / (25 * C)
        return total.reshape(TH, COLS, QUERIES) * lax.rsqrt(25 * C * (energy + 1e-05))[:, :, None]
    bands = lax.map(one_band, jnp.arange(N_LAT, dtype=jnp.int32))
    return bands.reshape(ROWS, COLS, QUERIES)
```

```python
import jax
import jax.numpy as jnp
from jax import lax
from jax.experimental import pallas as pl
from jax.experimental.pallas import tpu as pltpu
from jax.sharding import PartitionSpec as P

F32 = jnp.float32
BF16 = jnp.bfloat16
SLOTS = 26
EPS = 1e-05


def gather_kernel(own_ref, row_ref, col_ref, emb_ref, tab_ref, edge_ref, flat, tabf):
    here = lax.axis_index("lat") * lax.axis_size("lon") + lax.axis_index("lon")
    rows, cols, chans = emb_ref.shape
    panels, per_panel = own_ref.shape
    count = panels * per_panel

    @pl.loop(0, rows)
    def _(i):
        flat[pl.ds(pl.multiple_of(i * cols, cols), cols), :] = emb_ref[i].astype(F32)

    @pl.loop(0, SLOTS)
    def _(s):
        tabf[pl.ds(pl.multiple_of(s * count, count), count), :] = jnp.zeros((count, chans), F32)

    for side, first in ((0, 0), (1, cols - 2)):
        for c in range(2):
            edge_ref[side, c] = flat[pl.ds(first + c, rows, stride=cols), :].astype(BF16)

    for p in range(panels):

        @pl.loop(0, per_panel)
        def _(q):
            @pl.when(own_ref[p, q] == here)
            def _():
                base = row_ref[p, q] * cols + col_ref[p, q]
                for dy in range(5):
                    for dx in range(5):
                        tabf[pl.ds((dy * 5 + dx) * count + p * per_panel + q, 1), :] = flat[
                            pl.ds(base + dy * cols + dx, 1), :
                        ]

    @pl.loop(0, SLOTS)
    def _(s):
        tab_ref[s] = tabf[pl.ds(pl.multiple_of(s * count, count), count), :].astype(BF16)


def gather_table(owner, row, col, emb):
    rows, cols, chans = emb.shape
    count = owner.size
    smem = pl.BlockSpec(memory_space=pltpu.SMEM)
    vmem = pl.BlockSpec(memory_space=pltpu.VMEM)
    return pl.pallas_call(
        gather_kernel,
        out_shape=(
            jax.ShapeDtypeStruct((SLOTS, count, chans), BF16),
            jax.ShapeDtypeStruct((2, 2, rows, chans), BF16),
        ),
        in_specs=[smem, smem, smem, vmem],
        out_specs=(vmem, vmem),
        scratch_shapes=[
            pltpu.VMEM((rows * cols, chans), F32),
            pltpu.VMEM((SLOTS * count, chans), F32),
        ],
        compiler_params=pltpu.CompilerParams(vmem_limit_bytes=16 << 20),
        name="gather_table",
    )(owner, row, col, emb)


def score_kernel(q_ref, emb_ref, rowh_ref, colh_ref, corn_ref, out_ref, ext, shifted, qn, inv, band_sum):
    rows, cols, chans = emb_ref.shape
    count = q_ref.shape[1]
    band = lax.axis_index("lat")
    top = (band != 0).astype(F32)
    bottom = (band != lax.axis_size("lat") - 1).astype(F32)

    @pl.loop(0, rows)
    def _(i):
        ext[i + 2, 8 : 8 + cols, :] = emb_ref[i].astype(F32)

    for r in range(2):
        ext[r, 8 : 8 + cols, :] = rowh_ref[0, r].astype(F32) * top
        ext[rows + 2 + r, 8 : 8 + cols, :] = rowh_ref[1, r].astype(F32) * bottom
    for c in range(2):
        ext[2 : 2 + rows, 6 + c : 7 + c, :] = colh_ref[0, c].astype(F32)[:, None, :]
        ext[2 : 2 + rows, 8 + cols + c : 9 + cols + c, :] = colh_ref[1, c].astype(F32)[:, None, :]
        for side, at in ((0, 6 + c), (1, 8 + cols + c)):
            above = corn_ref[side, c].astype(F32) * top
            below = corn_ref[2 + side, c].astype(F32) * bottom
            for r in range(2):
                ext[r, at : at + 1, :] = above[6 + r : 7 + r]
                ext[rows + 2 + r, at : at + 1, :] = below[r : r + 1]

    @pl.loop(0, rows + 4)
    def _(i):
        for dx in range(5):
            shifted[i, :, dx * chans : (dx + 1) * chans] = ext[i, 6 + dx : 6 + dx + cols, :].astype(BF16)

    @pl.loop(0, rows)
    def _(i):
        column = jnp.zeros((cols + 16, chans), F32)
        for dy in range(5):
            column = column + jnp.square(ext[i + dy])
        band_sum[...] = column
        box = jnp.zeros((cols, chans), F32)
        for dx in range(5):
            box = box + band_sum[6 + dx : 6 + dx + cols, :]
        energy = jnp.sum(box, axis=1, keepdims=True) / (25 * chans)
        inv[i] = jnp.broadcast_to(lax.rsqrt(25 * chans * (energy + EPS)), (cols, chans))

    total = jnp.zeros((count, chans), F32)
    for s in range(25):
        total = total + jnp.square(q_ref[s].astype(F32))
    scale = lax.rsqrt(jnp.sum(total, axis=1, keepdims=True) / (25 * chans) + EPS)
    for s in range(25):
        qn[:, s * chans : (s + 1) * chans] = (q_ref[s].astype(F32) * scale).astype(BF16)

    block = 8

    @pl.loop(0, rows // block)
    def _(b):
        acc = jnp.zeros((block * cols, count), F32)
        for dy in range(5):
            lhs = shifted[pl.ds(b * block + dy, block)].reshape(block * cols, 5 * chans)
            rhs = qn[:, dy * 5 * chans : (dy + 1) * 5 * chans]
            acc = acc + lax.dot_general(lhs, rhs, (((1,), (1,)), ((), ())), preferred_element_type=F32)
        out_ref[pl.ds(b * block, block)] = acc.reshape(block, cols, count) * inv[pl.ds(b * block, block)]


def score(q, emb, rowh, colh, corn):
    rows, cols, chans = emb.shape
    count = q.shape[1]
    vmem = pl.BlockSpec(memory_space=pltpu.VMEM)
    return pl.pallas_call(
        score_kernel,
        out_shape=jax.ShapeDtypeStruct((rows, cols, count), F32),
        in_specs=[vmem] * 5,
        out_specs=vmem,
        scratch_shapes=[
            pltpu.VMEM((rows + 4, cols + 16, chans), F32),
            pltpu.VMEM((rows + 4, cols, 5 * chans), BF16),
            pltpu.VMEM((count, 25 * chans), BF16),
            pltpu.VMEM((rows, cols, chans), F32),
            pltpu.VMEM((cols + 16, chans), F32),
        ],
        compiler_params=pltpu.CompilerParams(vmem_limit_bytes=48 << 20),
        name="score",
    )(q, emb, rowh, colh, corn)


def body(embeddings, query_owner, query_row, query_col):
    table, edge = gather_table(query_owner, query_row, query_col, embeddings)
    queries = lax.psum(table, ("lon", "lat"))
    lon = lax.axis_size("lon")
    lat = lax.axis_size("lat")
    up = [(i, (i + 1) % lat) for i in range(lat)]
    down = [(j, i) for i, j in up]
    right = [(i, (i + 1) % lon) for i in range(lon)]
    left = [(j, i) for i, j in right]
    rowh = jnp.stack([lax.ppermute(embeddings[-2:], "lat", up), lax.ppermute(embeddings[:2], "lat", down)])
    colh = jnp.stack([lax.ppermute(edge[1], "lon", right), lax.ppermute(edge[0], "lon", left)])
    above = lax.ppermute(colh[:, :, -8:], "lat", up)
    below = lax.ppermute(colh[:, :, :8], "lat", down)
    return score(queries, embeddings, rowh, colh, jnp.concatenate([above, below]))


def solution(mesh):
    placed = (P("lat", "lon", None), P(), P(), P())
    return jax.shard_map(
        body, mesh=mesh, in_specs=placed, out_specs=P("lat", "lon", None), check_vma=False
    )
```
